32 devices in a mesh: seq: 8 (over z, x), head: 4 (over y, core).
Axes of the slice: x: 2, y: 2, z: 4, core: 2. Of those that a mesh axis runs over, the one named last changes fastest.
Arguments:
- features: bfloat16 [8192, 8192], P(('seq', 'head')), may hold values from -6 to 6
- gate_input: bfloat16 [8192, 8192], P(('seq', 'head')), may hold values from -6 to 6
- bmat: bfloat16 [8192, 8, 128], P(('seq', 'head')), may hold values from -1.78125 to 1.78125
- cmat: bfloat16 [8192, 8, 128], P(('seq', 'head')), may hold values from -1.78125 to 1.78125
- step_size: float32 [8192, 128], P(('seq', 'head')), may hold values from 0.001 to 0.1
- log_decay: float32 [8192, 128], P(('seq', 'head')), may hold values from -0.8 to 0
- skip: float32 [128], P('head'), may hold values from 0.5 to 2
- norm_gain: float32 [8192], replicated, may hold values from 0.1 to 1.9
Outputs:
- mixed: bfloat16 [8192, 8192], P(('seq', 'head'))
The draws below stay inside these ranges and needn't reach their ends.
All inputs are finite; a program needn't handle non-finite values.
Results may differ from the reference program's by a relative error of at most 0.0085.
Values may be sent and summed in bfloat16 or wider, within the bound.
No kernel may reach another device: no remote copies, remote signals or barrier semaphores. Data moves between devices by JAX's collectives and lax.ppermute only.
A program may use at most 128 MiB of HBM per device.

```python
import math
import jax
import jax.numpy as jnp
from jax import lax

HEAD_TOTAL = 128
HEADDIM = 64
STATE = 128
GROUPS = 8
SPAN = 256
TOKEN_LENGTH = 8192
INNER = 8192


def draw_log_decay(key, part):
    random_subkeys = jax.random.split(key, 6)
    fast_share = 0.5
    factor = jnp.exp(jax.random.uniform(random_subkeys[5], (TOKEN_LENGTH, HEAD_TOTAL), jnp.float32, -0.6931, 0.6931))
    fast_heads = jax.random.bernoulli(random_subkeys[0], fast_share, (HEAD_TOTAL,))
    fast_rate = jnp.exp(jax.random.uniform(random_subkeys[1], (HEAD_TOTAL,), jnp.float32, math.log(1.0 / 50.0), math.log(1.0 / 30.0)))
    slow_rate = jnp.exp(jax.random.uniform(random_subkeys[2], (HEAD_TOTAL,), jnp.float32, math.log(0.25), 0.0)) * (0.6931 / TOKEN_LENGTH)
    decay_rate_lookup = jnp.where(fast_heads, fast_rate, slow_rate)[None, :] * factor
    half_length = TOKEN_LENGTH // 2
    surge_offset = jax.random.randint(random_subkeys[3], (2, HEAD_TOTAL), 0, half_length)
    surge_location = surge_offset + jnp.array([0, half_length], jnp.int32)[:, None]
    surge_depth = jax.random.uniform(random_subkeys[4], (2, HEAD_TOTAL), jnp.float32, math.log(0.5), math.log(0.8))
    token_positions = jnp.arange(TOKEN_LENGTH)[:, None, None]
    surge_terms = jnp.sum(jnp.where(token_positions == surge_location[None], surge_depth[None], 0.0), axis=1)
    return (surge_terms - decay_rate_lookup).astype(jnp.float32)


def shard_levels(rng, dims, pieces, low, high):
    def one(axis_at, parts):
        heights = jax.random.uniform(jax.random.fold_in(jax.random.fold_in(rng, 6), axis_at), (parts,), jnp.float32, low / len(pieces), high / len(pieces))
        return jnp.repeat(jnp.exp(heights), dims[axis_at] // parts).reshape((-1,) + (1,) * (len(dims) - axis_at - 1))

    level = one(*pieces[0])
    for cut in pieces[1:]:
        level = level * one(*cut)
    return level


def normal_values(own_key, dims, scale, reach, cuts=(), held_as=jnp.bfloat16):
    values = jax.random.normal(own_key, dims, jnp.float32) * scale
    if len(cuts) > 0:
        values = shard_levels(own_key, dims, cuts, -0.22, 0.18) * values
    return jnp.clip(values, min=-reach, max=reach).astype(held_as)


def setup_inputs(seed: int = 0) -> dict:
    splits = jax.random.split(jax.random.key(seed), 9)
    return {
        "features": normal_values(splits[0], (TOKEN_LENGTH, INNER), 1.0, 6.0, ((0, 32),)),
        "gate_input": normal_values(splits[1], (TOKEN_LENGTH, INNER), 1.0, 6.0, ((0, 32),)),
        "bmat": normal_values(splits[2], (TOKEN_LENGTH, GROUPS, STATE), (STATE ** -0.25), 1.78125, ((0, 32),)),
        "cmat": normal_values(splits[3], (TOKEN_LENGTH, GROUPS, STATE), (STATE ** -0.25), 1.78125, ((0, 32),)),
        "step_size": jnp.clip(jnp.exp(math.log(0.1) - 4.6051702 * jax.random.uniform(splits[4], (TOKEN_LENGTH, HEAD_TOTAL), jnp.float32) ** shard_levels(splits[4], (TOKEN_LENGTH, HEAD_TOTAL), ((0, 32),), -0.2, 0.2)), 0.001, 0.1),
        "log_decay": draw_log_decay(jax.random.fold_in(splits[8], 71), 0),
        "skip": jnp.clip(0.5 + 1.5 * jax.random.uniform(splits[6], (HEAD_TOTAL,), jnp.float32) ** shard_levels(splits[6], (HEAD_TOTAL,), ((0, 4),), -0.2, 0.2), 0.5, 2.0),
        "norm_gain": jnp.clip(1.0 + 0.18 * jax.random.normal(splits[7], (INNER,), jnp.float32), 0.1, 1.9),
    }


def block_terms(feature_block, b_block, c_block, dt_block, cum_block):
    highest = lax.Precision.HIGHEST
    length = cum_block.shape[0]
    token_positions = jnp.arange(length)
    causal = token_positions[:, None] >= token_positions[None, :]
    scores = jnp.einsum('tgn,sgn->gts', c_block.astype(jnp.float32), b_block.astype(jnp.float32), precision=highest)
    cum_heads = jnp.transpose(cum_block, (1, 2, 0))
    spread = cum_heads[:, :, :, None] - cum_heads[:, :, None, :]
    step_scale = jnp.transpose(dt_block, (1, 2, 0))[:, :, None, :]
    weights = jnp.where(causal, scores[:, None] * jnp.exp(jnp.where(causal, spread, 0.0)) * step_scale, 0.0).astype(jnp.bfloat16)
    intra_terms = jnp.einsum('ghts,sghp->tghp', weights.astype(jnp.float32), feature_block.astype(jnp.float32), precision=highest)
    tail_scale = jnp.exp(cum_block[-1:] - cum_block) * dt_block
    loaded = (b_block[:, :, None, :].astype(jnp.float32) * tail_scale[..., None]).astype(jnp.bfloat16)
    update = jnp.einsum('sghn,sghp->ghpn', loaded.astype(jnp.float32), feature_block.astype(jnp.float32), precision=highest)
    return (intra_terms, update)

def normalize(values, gate_part, gain_row):
    gated_values = values.astype(jnp.float32) * jax.nn.silu(gate_part.astype(jnp.float32))
    inverse_rms = lax.rsqrt(lax.optimization_barrier(jnp.mean(gated_values * gated_values, axis=-1, keepdims=True)) + 1e-05)
    return (gated_values * inverse_rms * gain_row).astype(jnp.bfloat16)

def reference(features, gate_input, bmat, cmat, step_size, log_decay, skip, norm_gain):
    per_group = HEAD_TOTAL // GROUPS
    group_width = per_group * HEADDIM
    block_count = TOKEN_LENGTH // SPAN
    feature_blocks = features.reshape(block_count, SPAN, GROUPS, per_group, HEADDIM)
    gate_blocks = gate_input.reshape(block_count, SPAN, GROUPS, group_width)
    b_blocks = bmat.reshape(block_count, SPAN, GROUPS, STATE)
    c_blocks = cmat.reshape(block_count, SPAN, GROUPS, STATE)
    dt_blocks = step_size.reshape(block_count, SPAN, GROUPS, per_group)
    decay_blocks = log_decay.reshape(block_count, SPAN, GROUPS, per_group)
    skip_table = skip.reshape(GROUPS, per_group)
    gain_table = norm_gain.reshape(GROUPS, group_width)

    def advance(carry_state, members):
        feature_block, gate_block, b_block, c_block, dt_block, decay_block = members
        cum_block = jnp.cumsum(decay_block, axis=0)
        intra_terms, update = block_terms(feature_block, b_block, c_block, dt_block, cum_block)
        carried = jnp.einsum('tgn,ghpn->tghp', c_block.astype(jnp.float32), carry_state, precision=lax.Precision.HIGHEST) * jnp.exp(cum_block)[..., None]
        ssm_out = (intra_terms + carried + skip_table[None, :, :, None] * feature_block.astype(jnp.float32)).astype(jnp.bfloat16)
        result = normalize(ssm_out.reshape(SPAN, GROUPS, group_width), gate_block, gain_table)
        next_state = jnp.exp(cum_block[-1])[..., None, None] * carry_state + update
        return (next_state, result)
    start_state = jnp.zeros((GROUPS, per_group, HEADDIM, STATE), jnp.float32)
    _, outcome = lax.scan(advance, start_state, (feature_blocks, gate_blocks, b_blocks, c_blocks, dt_blocks, decay_blocks))
    return outcome.reshape(TOKEN_LENGTH, INNER)
```

```python
import jax
import jax.numpy as jnp
from jax import lax
from jax.experimental import pallas as pl
from jax.experimental.pallas import tpu as pltpu
from jax.sharding import PartitionSpec as P

SUB = 128
MID = SUB // 2 - 1
EXTRA = 16
PLANE = 4
AXES = ("seq", "head")
F32, BF16 = jnp.float32, jnp.bfloat16
VM = pl.BlockSpec(memory_space=pltpu.VMEM)
SM = pl.BlockSpec(memory_space=pltpu.SMEM)


def split_two(value):
    high = value.astype(BF16)
    return high, (value - high.astype(F32)).astype(BF16)


def dot(a, b):
    return lax.dot_general(a, b, (((1,), (0,)), ((), ())), preferred_element_type=F32)


def dot_tn(a, b):
    return lax.dot_general(a, b, (((0,), (0,)), ((), ())), preferred_element_type=F32)


def dot_nt(a, b):
    return lax.dot_general(a, b, (((1,), (1,)), ((), ())), preferred_element_type=F32)


def spread_matrix(group, heads, per_group, width):
    row = lax.broadcasted_iota(jnp.int32, (2 * heads, width), 0)
    column = lax.broadcasted_iota(jnp.int32, (2 * heads, width), 1)
    head = group * per_group + column // (width // per_group)
    return ((row == head) | (row == head + heads)).astype(BF16)


def pair_row(later, earlier, subs):
    return 1 + 2 * subs + later * (later - 1) // 2 + earlier


def decay_of(ref):
    rows = ref[-EXTRA:, :].astype(F32)
    return rows[0:1] + rows[1:2]


def put_decay(ref, decay):
    high, low = split_two(decay)
    row = lax.broadcasted_iota(jnp.int32, (EXTRA, decay.shape[1]), 0)
    both = jnp.where(row == 0, high.astype(F32), jnp.where(row == 1, low.astype(F32), 0.0))
    ref[-EXTRA:, :] = both.astype(BF16)


def write_scales(decay_ref, step_ref, sx_ref, sr_ref):
    rows, heads = decay_ref.shape
    subs = rows // SUB
    decay = decay_ref[...]
    high = decay.astype(BF16)
    rest = decay - high.astype(F32)
    mid = rest.astype(BF16)
    low = (rest - mid.astype(F32)).astype(BF16)
    row = lax.broadcasted_iota(jnp.int32, (rows, rows), 0)
    column = lax.broadcasted_iota(jnp.int32, (rows, rows), 1)
    lower = (row >= column).astype(BF16)
    cum = dot(lower, high) + dot(lower, mid) + dot(lower, low)
    centre = [cum[b * SUB + MID : b * SUB + MID + 1] for b in range(subs)]
    last = cum[rows - 1 : rows]
    for b in range(subs):
        part = slice(b * SUB, (b + 1) * SUB)
        off = cum[part] - centre[b]
        high, low = split_two(jnp.exp(-off) * step_ref[part, :])
        sx_ref[part, :heads] = high
        sx_ref[part, heads:] = low
        high, low = split_two(jnp.exp(off))
        sr_ref[part, :heads] = high
        sr_ref[part, heads:] = low
    scalars = [last] + [last - c for c in centre] + centre
    for b in range(subs):
        scalars += [centre[b] - centre[a] for a in range(b)]
    pad = jnp.zeros((EXTRA - len(scalars), heads), F32)
    high, low = split_two(jnp.exp(jnp.concatenate(scalars + [pad], axis=0)))
    sx_ref[rows:, :heads] = high
    sx_ref[rows:, heads:] = low


def scaled_features(x_ref, sx_ref, spread):
    rows = x_ref.shape[0]
    scale = dot(sx_ref[...], spread)
    return (x_ref[...].astype(F32) * scale[:rows]).astype(BF16), scale[rows:]


def update_of(xa, b_group, scalars, out_ref):
    rows = xa.shape[0]
    total = None
    for b in range(rows // SUB):
        part = slice(b * SUB, (b + 1) * SUB)
        term = dot_tn(b_group[part], xa[part]) * scalars[1 + b : 2 + b]
        total = term if total is None else total + term
    out_ref[:-EXTRA, :] = total.astype(BF16)
    put_decay(out_ref, scalars[0:1])


def first_kernel(ids, x_ref, b_ref, step_ref, decay_ref, u_ref, bg_ref, sx_ref, sr_ref, b32):
    i = pl.program_id(0)
    rows, groups, state = b_ref.shape
    heads = step_ref.shape[1]
    per_group = heads // groups

    @pl.when(i == 0)
    def _():
        write_scales(decay_ref, step_ref, sx_ref, sr_ref)
        b32[...] = b_ref[...].astype(F32).reshape(rows * groups, state)
        for g in range(groups):
            bg_ref[g] = b32[pl.ds(g, rows, stride=groups), :].astype(BF16)

    group = ids[0] + i
    spread = spread_matrix(group, heads, per_group, x_ref.shape[1])
    xa, scalars = scaled_features(x_ref, sx_ref, spread)
    update_of(xa, bg_ref[group], scalars, u_ref.at[0])


def second_kernel(ids, x_ref, bg_ref, sx_ref, u_ref):
    groups = bg_ref.shape[0]
    heads = sx_ref.shape[1] // 2
    group = ids[1] + pl.program_id(0)
    spread = spread_matrix(group, heads, heads // groups, x_ref.shape[1])
    xa, scalars = scaled_features(x_ref, sx_ref, spread)
    update_of(xa, bg_ref[group], scalars, u_ref.at[0])


def local_kernel(x_ref, c_ref, bg_ref, sx_ref, sr_ref, skip_ref, y_ref, cg_ref, c32):
    group = pl.program_id(0)
    rows, groups, state = c_ref.shape
    heads = sx_ref.shape[1] // 2
    subs = rows // SUB

    @pl.when(group == 0)
    def _():
        c32[...] = c_ref[...].astype(F32).reshape(rows * groups, state)
        for g in range(groups):
            cg_ref[g] = c32[pl.ds(g, rows, stride=groups), :].astype(BF16)

    spread = spread_matrix(group, heads, heads // groups, x_ref.shape[1])
    xa, scalars = scaled_features(x_ref, sx_ref, spread)
    row_scale = dot(sr_ref[...], spread)
    high, low = split_two(jnp.broadcast_to(skip_ref[...], (EXTRA, heads)))
    skip = dot(jnp.concatenate([high, low], axis=1), spread)[0:1]
    row = lax.broadcasted_iota(jnp.int32, (SUB, SUB), 0)
    column = lax.broadcasted_iota(jnp.int32, (SUB, SUB), 1)
    b_group, c_group = bg_ref[group], cg_ref[group]
    for b in range(subs):
        part = slice(b * SUB, (b + 1) * SUB)
        scores = jnp.where(row >= column, dot_nt(c_group[part], b_group[part]), 0.0)
        inner = dot(scores.astype(BF16), xa[part])
        for a in range(b):
            other = slice(a * SUB, (a + 1) * SUB)
            scores = dot_nt(c_group[part], b_group[other]).astype(BF16)
            at = pair_row(b, a, subs)
            inner = inner + dot(scores, xa[other]) * scalars[at : at + 1]
        y_ref[part, :] = row_scale[part] * inner + skip * x_ref[part, :].astype(F32)


def pair_down_kernel(ids, own_ref, far_ref, *outs):
    core, chip = ids[2], ids[3]

    def run(first, second):
        for m in range(PLANE):
            slot = chip ^ m
            d0, d1 = decay_of(first.at[slot]), decay_of(second.at[slot])
            u0, u1 = first[slot, :-EXTRA, :], second[slot, :-EXTRA, :]
            outs[m][:-EXTRA, :] = (d1 * u0.astype(F32) + u1.astype(F32)).astype(BF16)
            put_decay(outs[m], d0 * d1)

    pl.when(core == 0)(lambda: run(own_ref, far_ref))
    pl.when(core == 1)(lambda: run(far_ref, own_ref))


def plane_down_kernel(ids, p0, p1, p2, p3, near_ref, away_ref, held):
    chip, side = ids[3], ids[4]
    for m, piece in enumerate((p0, p1, p2, p3)):
        held[chip ^ m] = piece[...]
    total, decay = held[0, :-EXTRA, :].astype(F32), decay_of(held.at[0])
    for k in range(1, PLANE):
        d = decay_of(held.at[k])
        total = d * total + held[k, :-EXTRA, :].astype(F32)
        decay = d * decay
    half = total.shape[1] // 2

    def put(low_ref, high_ref):
        low_ref[:-EXTRA, :] = total[:, :half].astype(BF16)
        high_ref[:-EXTRA, :] = total[:, half:].astype(BF16)
        put_decay(low_ref, decay[:, :half])
        put_decay(high_ref, decay[:, half:])

    pl.when(side == 0)(lambda: put(near_ref, away_ref))
    pl.when(side == 1)(lambda: put(away_ref, near_ref))


def side_down_kernel(ids, own_ref, far_ref, out_ref):
    def run(first, second):
        d0, d1 = decay_of(first), decay_of(second)
        out_ref[:-EXTRA, :] = (
            d1 * first[:-EXTRA, :].astype(F32) + second[:-EXTRA, :].astype(F32)
        ).astype(BF16)
        put_decay(out_ref, d0 * d1)

    pl.when(ids[4] == 0)(lambda: run(own_ref, far_ref))
    pl.when(ids[4] == 1)(lambda: run(far_ref, own_ref))


def side_up_kernel(ids, enter_ref, own_ref, far_ref, near_ref, away_ref):
    enter = enter_ref[:-EXTRA, :]

    def run(first, first_out, second_out):
        first_out[...] = enter
        after = decay_of(first) * enter.astype(F32) + first[:-EXTRA, :].astype(F32)
        second_out[...] = after.astype(BF16)

    pl.when(ids[4] == 0)(lambda: run(own_ref, near_ref, away_ref))
    pl.when(ids[4] == 1)(lambda: run(far_ref, away_ref, near_ref))


def plane_up_kernel(ids, near_ref, away_ref, p0, p1, p2, p3, o0, o1, o2, o3, held, state):
    chip, side = ids[3], ids[4]
    half = near_ref.shape[1]
    for m, piece in enumerate((p0, p1, p2, p3)):
        held[chip ^ m] = piece[...]

    def enter(low_ref, high_ref):
        state[0, :, :half] = low_ref[...]
        state[0, :, half:] = high_ref[...]

    pl.when(side == 0)(lambda: enter(near_ref, away_ref))
    pl.when(side == 1)(lambda: enter(away_ref, near_ref))
    now = state[0].astype(F32)
    for k in range(1, PLANE):
        now = decay_of(held.at[k - 1]) * now + held[k - 1, :-EXTRA, :].astype(F32)
        state[k] = now.astype(BF16)
    for m, out in enumerate((o0, o1, o2, o3)):
        out[...] = state[chip ^ m]


def pair_up_kernel(ids, own_ref, far_ref, s0, s1, s2, s3, mine_ref, send_ref):
    core, chip = ids[2], ids[3]

    def run(first, first_out, second_out):
        for m, piece in enumerate((s0, s1, s2, s3)):
            slot = chip ^ m
            first_out[slot] = piece[...]
            after = decay_of(first.at[slot]) * piece[...].astype(F32)
            second_out[slot] = (after + first[slot, :-EXTRA, :].astype(F32)).astype(BF16)

    pl.when(core == 0)(lambda: run(own_ref, mine_ref, send_ref))
    pl.when(core == 1)(lambda: run(far_ref, send_ref, mine_ref))


def small_call(kernel, ids, args, outs, scratch=()):
    size = sum(a.size * 2 for a in args) + sum(2 * o.size for o in outs)
    return pl.pallas_call(
        kernel,
        out_shape=outs,
        in_specs=[SM] + [VM] * len(args),
        out_specs=[VM] * len(outs),
        scratch_shapes=list(scratch),
        cost_estimate=pl.CostEstimate(flops=size, bytes_accessed=size, transcendentals=0),
    )(ids, *args)


def exchange(value, mask, count):
    return lax.ppermute(value, AXES, [(i, i ^ mask) for i in range(count)])


def shifted(value, steps, count):
    return lax.ppermute(value, AXES, [(i, i + steps) for i in range(count - steps)])


def scan_groups(total, stride, count):
    places = count // stride

    def parts(message):
        decay = message[-EXTRA].astype(F32) + message[-EXTRA + 1].astype(F32)
        return message[:-EXTRA].astype(F32), decay

    def packed(value, decay):
        high, low = split_two(decay)
        rest = jnp.zeros((EXTRA - 2, decay.shape[0]), BF16)
        return jnp.concatenate([value.astype(BF16), high[None], low[None], rest], axis=0)

    covered = shifted(total, stride, count)
    reach = 1
    while reach < places - 1:
        value, decay = parts(covered)
        own, own_decay = parts(total)
        longer = packed(own_decay[None] * value + own, own_decay * decay)
        far, far_decay = parts(shifted(longer, stride * (reach + 1), count))
        covered = packed(decay[None] * far + value, decay * far_decay)
        reach = 2 * reach + 1
    return covered


def finish(group, y_ref, cg_ref, sx_ref, sr_ref, s_ref, gate_ref, gain_ref, out_ref):
    rows, width = y_ref.shape
    groups = cg_ref.shape[0]
    heads = sx_ref.shape[1] // 2
    subs = rows // SUB
    spread = spread_matrix(group, heads, heads // groups, width)
    row_scale = dot(sr_ref[...], spread)
    scalars = dot(sx_ref[rows:, :], spread)
    c_group, state = cg_ref[group], s_ref[0]
    for b in range(subs):
        part = slice(b * SUB, (b + 1) * SUB)
        at = 1 + subs + b
        carried = dot(c_group[part], state) * scalars[at : at + 1]
        ssm = (y_ref[part, :] + row_scale[part] * carried).astype(BF16).astype(F32)
        gate = gate_ref[part, :].astype(F32)
        gated = ssm * (gate / (1.0 + jnp.exp(-gate)))
        mean = jnp.mean(gated * gated, axis=1, keepdims=True)
        out_ref[part, :] = (gated * lax.rsqrt(mean + 1e-05) * gain_ref[...]).astype(BF16)


def own_finish_kernel(ids, *refs):
    finish(ids[1] + pl.program_id(0), *refs)


def far_finish_kernel(ids, *refs):
    finish(ids[0] + pl.program_id(0), *refs[:-2], refs[-1])


def shards(features, gate_input, bmat, cmat, step_size, log_decay, skip, norm_gain):
    rows, inner = features.shape
    groups, state = bmat.shape[1:]
    heads = step_size.shape[1]
    width = inner // groups
    half = groups // 2
    count = lax.axis_size("seq") * lax.axis_size("head")
    me = lax.axis_index("seq") * lax.axis_size("head") + lax.axis_index("head")
    core = me & 1
    chip = (me >> 1) & (PLANE - 1)
    side = (me >> 3) & 1
    ids = jnp.stack([(1 - core) * half, core * half, core, chip, side]).astype(jnp.int32)
    tall = state + EXTRA

    def out(*shape, kind=BF16):
        return jax.ShapeDtypeStruct(shape, kind)

    def whole(*shape):
        return pl.BlockSpec(shape, lambda i, *_: (0,) * len(shape))

    def cols(which):
        return pl.BlockSpec((rows, width), lambda i, ids: (0, ids[which] + i))

    slot_spec = pl.BlockSpec((1, tall, width), lambda i, *_: (i, 0, 0))
    grid = pltpu.PrefetchScalarGridSpec
    small = whole(rows + EXTRA, 2 * heads)
    away, bg, sx, sr = pl.pallas_call(
        first_kernel,
        grid_spec=grid(
            num_scalar_prefetch=1,
            grid=(half,),
            in_specs=[cols(0), whole(rows, groups, state), whole(rows, heads), whole(rows, heads)],
            out_specs=[slot_spec, whole(groups, rows, state), small, whole(rows, 2 * heads)],
            scratch_shapes=[pltpu.VMEM((rows * groups, state), F32)],
        ),
        out_shape=[
            out(half, tall, width),
            out(groups, rows, state),
            out(rows + EXTRA, 2 * heads),
            out(rows, 2 * heads),
        ],
        cost_estimate=pl.CostEstimate(flops=10**9, bytes_accessed=8 * 2**20, transcendentals=0),
    )(ids, features, bmat, step_size, log_decay)
    pair_far = exchange(away, 1, count)
    (pair_own,) = pl.pallas_call(
        second_kernel,
        grid_spec=grid(
            num_scalar_prefetch=1,
            grid=(half,),
            in_specs=[cols(1), whole(groups, rows, state), small],
            out_specs=[slot_spec],
        ),
        out_shape=[out(half, tall, width)],
        cost_estimate=pl.CostEstimate(flops=10**9, bytes_accessed=8 * 2**20, transcendentals=0),
    )(ids, features, bg, sx)

    pieces = small_call(pair_down_kernel, ids, (pair_own, pair_far), [out(tall, width)] * PLANE)
    pieces = [pieces[0]] + [exchange(pieces[m], 2 * m, count) for m in range(1, PLANE)]

    skips = skip
    for bit in range((heads // skip.shape[0]).bit_length() - 1):
        other = exchange(skips, 1 << bit, count)
        first = (lax.axis_index("head") >> bit) & 1 == 0
        skips = jnp.where(first, jnp.concatenate([skips, other]), jnp.concatenate([other, skips]))
    local, cg = pl.pallas_call(
        local_kernel,
        grid=(groups,),
        in_specs=[
            pl.BlockSpec((rows, width), lambda i: (0, i)),
            whole(rows, groups, state),
            whole(groups, rows, state),
            small,
            whole(rows, 2 * heads),
            whole(1, heads),
        ],
        out_specs=[pl.BlockSpec((rows, width), lambda i: (0, i)), whole(groups, rows, state)],
        out_shape=[out(rows, inner, kind=F32), out(groups, rows, state)],
        scratch_shapes=[pltpu.VMEM((rows * groups, state), F32)],
        cost_estimate=pl.CostEstimate(flops=10**10, bytes_accessed=16 * 2**20, transcendentals=0),
    )(features, cmat, bg, sx, sr, skips.reshape(1, heads))

    side_own, side_send = small_call(
        plane_down_kernel,
        ids,
        pieces,
        [out(tall, width // 2)] * 2,
        [pltpu.VMEM((PLANE, tall, width), BF16)],
    )
    side_far = exchange(side_send, 8, count)
    (total,) = small_call(side_down_kernel, ids, (side_own, side_far), [out(tall, width // 2)])
    enter = scan_groups(total, 16, count)
    near, send = small_call(
        side_up_kernel, ids, (enter, side_own, side_far), [out(state, width // 2)] * 2
    )
    far = exchange(send, 8, count)
    states = small_call(
        plane_up_kernel,
        ids,
        (near, far, *pieces),
        [out(state, width)] * PLANE,
        [pltpu.VMEM((PLANE, tall, width), BF16), pltpu.VMEM((PLANE, state, width), BF16)],
    )
    states = [states[0]] + [exchange(states[m], 2 * m, count) for m in range(1, PLANE)]
    mine, send = small_call(
        pair_up_kernel, ids, (pair_own, pair_far, *states), [out(half, state, width)] * 2
    )
    theirs = exchange(send, 1, count)

    def finish_specs(which):
        return [
            cols(which),
            whole(groups, rows, state),
            small,
            whole(rows, 2 * heads),
            pl.BlockSpec((1, state, width), lambda i, ids: (i, 0, 0)),
            cols(which),
            pl.BlockSpec((1, width), lambda i, ids: (0, ids[which] + i)),
        ]

    gain = norm_gain.reshape(1, inner)
    cost = pl.CostEstimate(flops=10**9, bytes_accessed=10 * 2**20, transcendentals=0)
    (result,) = pl.pallas_call(
        own_finish_kernel,
        grid_spec=grid(
            num_scalar_prefetch=1, grid=(half,), in_specs=finish_specs(1), out_specs=[cols(1)]
        ),
        out_shape=[out(rows, inner)],
        cost_estimate=cost,
    )(ids, local, cg, sx, sr, mine, gate_input, gain)
    (result,) = pl.pallas_call(
        far_finish_kernel,
        grid_spec=grid(
            num_scalar_prefetch=1,
            grid=(half,),
            in_specs=finish_specs(0) + [pl.BlockSpec(memory_space=pl.ANY)],
            out_specs=[cols(0)],
        ),
        out_shape=[out(rows, inner)],
        input_output_aliases={8: 0},
        cost_estimate=cost,
    )(ids, local, cg, sx, sr, theirs, gate_input, gain, result)
    return result


def solution(mesh):
    return jax.shard_map(
        shards,
        mesh=mesh,
        in_specs=(
            P(("seq", "head"), None),
            P(("seq", "head"), None),
            P(("seq", "head"), None, None),
            P(("seq", "head"), None, None),
            P(("seq", "head"), None),
            P(("seq", "head"), None),
            P("head"),
            P(),
        ),
        out_specs=P(("seq", "head"), None),
        check_vma=False,
    )
```

```python
import jax
import jax.numpy as jnp
import numpy as np
from jax import lax
from jax.experimental import pallas as pl
from jax.experimental.pallas import tpu as pltpu
from jax.sharding import PartitionSpec as P

SUB = 128
MID = SUB // 2 - 1
EXTRA = 8
PLANE = 4
AXES = ("seq", "head")
MIB = 2**20
F32, BF16 = jnp.float32, jnp.bfloat16
VM = pl.BlockSpec(memory_space=pltpu.VMEM)
SM = pl.BlockSpec(memory_space=pltpu.SMEM)
ANY = pl.BlockSpec(memory_space=pl.ANY)
CORE, CHIP, SIDE = 0, 1, 2


def split_two(value):
    high = value.astype(BF16)
    return high, (value - high.astype(F32)).astype(BF16)


def dot(a, b):
    return lax.dot_general(a, b, (((1,), (0,)), ((), ())), preferred_element_type=F32)


def dot_tn(a, b):
    return lax.dot_general(a, b, (((0,), (0,)), ((), ())), preferred_element_type=F32)


def dot_nt(a, b):
    return lax.dot_general(a, b, (((1,), (1,)), ((), ())), preferred_element_type=F32)


def spread_table(heads, groups, width):
    per_group = heads // groups
    row = np.arange(3 * heads - per_group)[:, None] % heads
    column = np.arange(width)[None, :] // (width // per_group)
    return jnp.asarray(row == heads - per_group + column, BF16)


def spread_of(table_ref, group, heads, groups):
    per_group = heads // groups
    start = pl.multiple_of(per_group * (groups - 1 - group), per_group)
    return table_ref[pl.ds(start, 2 * heads), :]


def pair_row(later, earlier, subs):
    return 1 + 2 * subs + later * (later - 1) // 2 + earlier


def decay_of(ref):
    rows = ref[-EXTRA:, :].astype(F32)
    return rows[0:1] + rows[1:2]


def put_decay(ref, decay):
    high, low = split_two(decay)
    row = lax.broadcasted_iota(jnp.int32, (EXTRA, decay.shape[1]), 0)
    both = jnp.where(row == 0, high.astype(F32), jnp.where(row == 1, low.astype(F32), 0.0))
    ref[-EXTRA:, :] = both.astype(BF16)


def write_scales(decay_ref, step_ref, sx_ref, sr_ref, sc_ref):
    rows, heads = decay_ref.shape
    subs = rows // SUB
    decay = decay_ref[...]
    high = decay.astype(BF16)
    rest = decay - high.astype(F32)
    mid = rest.astype(BF16)
    low = (rest - mid.astype(F32)).astype(BF16)
    row = lax.broadcasted_iota(jnp.int32, (rows, rows), 0)
    column = lax.broadcasted_iota(jnp.int32, (rows, rows), 1)
    lower = (row >= column).astype(BF16)
    cum = dot(lower, high) + dot(lower, mid) + dot(lower, low)
    centre = [cum[b * SUB + MID : b * SUB + MID + 1] for b in range(subs)]
    last = cum[rows - 1 : rows]
    for b in range(subs):
        part = slice(b * SUB, (b + 1) * SUB)
        off = cum[part] - centre[b]
        high, low = split_two(jnp.exp(-off) * step_ref[part, :])
        sx_ref[part, :heads] = high
        sx_ref[part, heads:] = low
        high, low = split_two(jnp.exp(off))
        sr_ref[part, :heads] = high
        sr_ref[part, heads:] = low
    scalars = [last] + [last - c for c in centre] + centre
    for b in range(subs):
        scalars += [centre[b] - centre[a] for a in range(b)]
    pad = jnp.zeros((EXTRA - len(scalars), heads), F32)
    high, low = split_two(jnp.exp(jnp.concatenate(scalars + [pad], axis=0)))
    sc_ref[:, :heads] = high
    sc_ref[:, heads:] = low


def scaled_features(x_ref, sx_ref, spread):
    return (x_ref[...].astype(F32) * dot(sx_ref[...], spread)).astype(BF16)


def update_of(xa, b_group, scalars):
    total = None
    for b in range(xa.shape[0] // SUB):
        part = slice(b * SUB, (b + 1) * SUB)
        term = dot_tn(b_group[part], xa[part]) * scalars[1 + b : 2 + b]
        total = term if total is None else total + term
    return total


def own_update(group, x_ref, bg_ref, sx_ref, sc_ref, table_ref):
    groups = bg_ref.shape[0]
    spread = spread_of(table_ref, group, sx_ref.shape[1] // 2, groups)
    scalars = dot(sc_ref[...], spread)
    return update_of(scaled_features(x_ref, sx_ref, spread), bg_ref[group], scalars), scalars[0:1]


def away_group(ids, slot, groups):
    return (1 - ids[CORE]) * (groups // 2) + (ids[CHIP] ^ slot)


def home_group(ids, slot, groups):
    return ids[CORE] * (groups // 2) + (ids[CHIP] ^ slot)


def put_update(ref, update, decay):
    ref[:-EXTRA, :] = update.astype(BF16)
    put_decay(ref, decay)


def first_kernel(
    ids, x_ref, b_ref, step_ref, decay_ref, table_ref, u_ref, bg_ref, sx_ref, sr_ref, sc_ref, b32
):
    i = pl.program_id(0)
    rows, groups, state = b_ref.shape

    @pl.when(i == 0)
    def _():
        write_scales(decay_ref, step_ref, sx_ref, sr_ref, sc_ref)
        b32[...] = b_ref[...].astype(F32).reshape(rows * groups, state)
        for g in range(groups):
            bg_ref[g] = b32[pl.ds(g, rows, stride=groups), :].astype(BF16)

    group = away_group(ids, 3 - i, groups)
    put_update(u_ref.at[0], *own_update(group, x_ref, bg_ref, sx_ref, sc_ref, table_ref))


def second_kernel(ids, x_ref, bg_ref, sx_ref, sc_ref, table_ref, u_ref):
    group = away_group(ids, 1 - pl.program_id(0), bg_ref.shape[0])
    put_update(u_ref.at[0], *own_update(group, x_ref, bg_ref, sx_ref, sc_ref, table_ref))


def home_kernel(slot, ids, x_ref, bg_ref, sx_ref, sc_ref, table_ref, far_ref, u_ref, p0, p1):
    i = pl.program_id(0)
    group = home_group(ids, slot - i, bg_ref.shape[0])
    update, decay = own_update(group, x_ref, bg_ref, sx_ref, sc_ref, table_ref)
    put_update(u_ref.at[0], update, decay)
    far, far_decay = far_ref[0, :-EXTRA, :].astype(F32), decay_of(far_ref.at[0])
    late = ids[CORE].astype(F32)
    joined = update * (late + (1.0 - late) * far_decay) + far * ((1.0 - late) + late * decay)
    both = decay * far_decay
    pl.when(i == 0)(lambda: put_update(p0, joined, both))
    pl.when(i == 1)(lambda: put_update(p1, joined, both))


def skip_kernel(ids, *refs):
    pieces, out_ref = refs[:-2], refs[-1]
    groups, _, width = out_ref.shape
    share = pieces[0].shape[1]
    heads = share * len(pieces)
    own = 2 * ids[CHIP] + ids[CORE]
    place = own & (len(pieces) - 1)
    row = lax.broadcasted_iota(jnp.int32, (share, width), 0)
    column = lax.broadcasted_iota(jnp.int32, (share, width), 1) // (width * groups // heads)
    spread_groups = share * groups // heads
    for m, piece in enumerate(pieces):
        high, low = split_two(jnp.broadcast_to(piece[...], (EXTRA, share)))
        for k in range(spread_groups):
            pick = (row == column + k * (heads // groups)).astype(BF16)
            out_ref[(place ^ m) * spread_groups + k] = dot(high, pick) + dot(low, pick)


def gate_kernel(gate_ref, out_ref):
    half = 0.5 * gate_ref[...].astype(F32)
    out_ref[0] = half + half * jnp.tanh(half)


def local_kernel(
    ids, x_ref, c_ref, bg_ref, sx_ref, sr_ref, sc_ref, table_ref, y_ref, r_ref, cg_ref, c32
):
    i = pl.program_id(0)
    group = i
    rows, groups, state = c_ref.shape
    heads = sx_ref.shape[1] // 2
    subs = rows // SUB

    @pl.when(i == 0)
    def _():
        c32[...] = c_ref[...].astype(F32).reshape(rows * groups, state)

    c_group = c32[pl.ds(group, rows, stride=groups), :].astype(BF16)
    cg_ref[0] = c_group
    spread = spread_of(table_ref, group, heads, groups)
    scalars = dot(sc_ref[...], spread)
    xa = scaled_features(x_ref, sx_ref, spread)
    row_scale = dot(sr_ref[...], spread)
    row = lax.broadcasted_iota(jnp.int32, (SUB, SUB), 0)
    column = lax.broadcasted_iota(jnp.int32, (SUB, SUB), 1)
    b_group = bg_ref[group]
    for b in range(subs):
        part = slice(b * SUB, (b + 1) * SUB)
        scores = jnp.where(row >= column, dot_nt(c_group[part], b_group[part]), 0.0)
        inner = dot(scores.astype(BF16), xa[part])
        for a in range(b):
            other = slice(a * SUB, (a + 1) * SUB)
            scores = dot_nt(c_group[part], b_group[other]).astype(BF16)
            at = pair_row(b, a, subs)
            inner = inner + dot(scores, xa[other]) * scalars[at : at + 1]
        y_ref[0, part, :] = row_scale[part] * inner
        r_ref[0, part, :] = row_scale[part] * scalars[1 + subs + b : 2 + subs + b]


def hold(held, place, pieces):
    for m, piece in enumerate(pieces):
        held[place ^ m] = piece[...]


def fold(held):
    total, decay = held[0, :-EXTRA, :].astype(F32), decay_of(held.at[0])
    for k in range(1, PLANE):
        d = decay_of(held.at[k])
        total = d * total + held[k, :-EXTRA, :].astype(F32)
        decay = d * decay
    return total, decay


def plane_down_kernel(ids, p0, p1, p2, p3, *refs):
    o0, o1, o2, o3, held, cut = refs[-6:]
    hold(held, ids[CHIP], (p0, p1, p2, p3))
    total, decay = fold(held)
    quarter = total.shape[1] // PLANE
    for k in range(PLANE):
        part = slice(k * quarter, (k + 1) * quarter)
        put_update(cut.at[k], total[:, part], decay[:, part])
    for m, out in enumerate((o0, o1, o2, o3)):
        out[...] = cut[ids[SIDE] ^ m]


def side_total_kernel(ids, p0, p1, p2, p3, out_ref, held):
    hold(held, ids[SIDE], (p0, p1, p2, p3))
    put_update(out_ref, *fold(held))


def side_up_kernel(ids, p0, p1, p2, p3, *refs):
    o0, o1, o2, o3, held, state = refs[-6:]
    hold(held, ids[SIDE], (p0, p1, p2, p3))
    if len(refs) == 8:
        state[0] = refs[0][:-EXTRA, :]
    else:
        state[0] = jnp.zeros(state.shape[1:], BF16)
    states_after(held, state)
    for m, out in enumerate((o0, o1, o2, o3)):
        out[...] = state[ids[SIDE] ^ m]


def states_after(held, state):
    now = state[0].astype(F32)
    for k in range(1, PLANE):
        now = decay_of(held.at[k - 1]) * now + held[k - 1, :-EXTRA, :].astype(F32)
        state[k] = now.astype(BF16)


def plane_up_kernel(ids, e0, e1, e2, e3, p0, p1, p2, p3, *refs):
    o0, o1, o2, o3, held, state, enter = refs[-7:]
    quarter = e0.shape[1]
    hold(held, ids[CHIP], (p0, p1, p2, p3))
    for m, piece in enumerate((e0, e1, e2, e3)):
        enter[ids[SIDE] ^ m] = piece[...]
    for k in range(PLANE):
        state[0, :, k * quarter : (k + 1) * quarter] = enter[k]
    states_after(held, state)
    for m, out in enumerate((o0, o1, o2, o3)):
        out[...] = state[ids[CHIP] ^ m]


def small_call(kernel, ids, args, outs, scratch=(), after=()):
    size = sum(a.size * 2 for a in args) + sum(2 * o.size for o in outs)
    return pl.pallas_call(
        kernel,
        out_shape=outs,
        in_specs=[SM] + [VM] * len(args) + [ANY] * len(after),
        out_specs=[VM] * len(outs),
        scratch_shapes=list(scratch),
        compiler_params=pltpu.CompilerParams(vmem_limit_bytes=8 * MIB),
        cost_estimate=pl.CostEstimate(flops=size, bytes_accessed=size, transcendentals=0),
    )(ids, *args, *after)


def exchange(value, mask, count):
    return lax.ppermute(value, AXES, [(i, i ^ mask) for i in range(count)])


def exchange_pieces(pieces, mask, count):
    moved = {}
    for m in (3, 2, 1):
        moved[m] = exchange(pieces[m], mask * m, count)
    return [pieces[0], moved[1], moved[2], moved[3]]


def shifted(value, steps, count):
    return lax.ppermute(value, AXES, [(i, i + steps) for i in range(count - steps)])


def scan_groups(total, stride, count):
    places = count // stride

    def parts(message):
        decay = message[-EXTRA].astype(F32) + message[-EXTRA + 1].astype(F32)
        return message[:-EXTRA].astype(F32), decay

    def packed(value, decay):
        high, low = split_two(decay)
        rest = jnp.zeros((EXTRA - 2, decay.shape[0]), BF16)
        return jnp.concatenate([value.astype(BF16), high[None], low[None], rest], axis=0)

    covered = shifted(total, stride, count)
    reach = 1
    while reach < places - 1:
        value, decay = parts(covered)
        own, own_decay = parts(total)
        longer = packed(own_decay[None] * value + own, own_decay * decay)
        far, far_decay = parts(shifted(longer, stride * (reach + 1), count))
        covered = packed(decay[None] * far + value, decay * far_decay)
        reach = 2 * reach + 1
    return covered


def finish_kernel(entries, ids, x_ref, y_ref, r_ref, gate_ref, cg_ref, gain_ref, skip_ref, *refs):
    count = len(entries)
    states, updates = refs[:count], refs[count : 2 * count]
    out_ref, held, made, sems = refs[-4:]
    groups, rows, width = y_ref.shape
    copies = []
    for n, (slot, side, at) in enumerate(entries):
        group = (ids[CORE] ^ side) * (groups // 2) + (ids[CHIP] ^ slot)

        @pl.when(ids[CORE] == 0)
        def _():
            held[n] = states[n][...]

        @pl.when(ids[CORE] == 1)
        def _():
            after = decay_of(updates[n].at[at]) * states[n][...].astype(F32)
            held[n] = (after + updates[n][at, :-EXTRA, :].astype(F32)).astype(BF16)

        columns = pl.ds(pl.multiple_of(group * width, width), width)
        gain, skip = gain_ref[:, columns], skip_ref[group, 0:1, :]
        for b in range(rows // SUB):
            part = slice(b * SUB, (b + 1) * SUB)
            carried = dot(cg_ref[group, part, :], held[n])
            ssm = y_ref[group, part, :] + r_ref[group, part, :] * carried
            ssm = (ssm + skip * x_ref[part, columns].astype(F32)).astype(BF16)
            gated = ssm.astype(F32) * gate_ref[group, part, :]
            mean = jnp.mean(gated * gated, axis=1, keepdims=True)
            made[n, part, :] = (gated * lax.rsqrt(mean + 1e-05) * gain).astype(BF16)
            copies.append(
                pltpu.make_async_copy(
                    made.at[n, part, :], out_ref.at[part, columns], sems.at[n, b]
                )
            )
            copies[-1].start()
    for copy in copies:
        copy.wait()


def shards(features, gate_input, bmat, cmat, step_size, log_decay, skip, norm_gain):
    rows, inner = features.shape
    groups, state = bmat.shape[1:]
    heads = step_size.shape[1]
    width = inner // groups
    count = lax.axis_size("seq") * lax.axis_size("head")
    me = lax.axis_index("seq") * lax.axis_size("head") + lax.axis_index("head")
    ids = jnp.stack([me & 1, (me >> 1) & (PLANE - 1), (me >> 3) & (PLANE - 1)]).astype(jnp.int32)
    tall = state + EXTRA
    table = spread_table(heads, groups, width)

    def far_memory(*values):
        return tuple(pltpu.with_memory_space_constraint(v, pltpu.HBM) for v in values)


    def out(*shape, kind=BF16):
        return jax.ShapeDtypeStruct(shape, kind)

    def whole(*shape):
        return pl.BlockSpec(shape, lambda i, *_: (0,) * len(shape))

    def block(place):
        return pl.BlockSpec((rows, width), lambda i, ids: (0, place(ids, i)))

    def call(kernel, steps, in_specs, out_specs, outs, args, scratch=(), aliases=None, cost=1, grant=8):
        return pl.pallas_call(
            kernel,
            grid_spec=pltpu.PrefetchScalarGridSpec(
                num_scalar_prefetch=1,
                grid=(steps,),
                in_specs=in_specs,
                out_specs=out_specs,
                scratch_shapes=list(scratch),
            ),
            out_shape=outs,
            input_output_aliases=aliases or {},
            compiler_params=pltpu.CompilerParams(vmem_limit_bytes=grant * MIB),
            cost_estimate=pl.CostEstimate(
                flops=cost * 10**9, bytes_accessed=cost * 4 * 2**20, transcendentals=0
            ),
        )(ids, *args)

    slot_spec = pl.BlockSpec((1, tall, width), lambda i, *_: (i, 0, 0))
    sx_spec, sc_spec = whole(rows, 2 * heads), whole(EXTRA, 2 * heads)
    table_spec, bg_spec = whole(*table.shape), whole(groups, rows, state)
    chunk = out(2, tall, width)

    away32, bg, sx, sr, sc = call(
        first_kernel,
        2,
        [
            block(lambda ids, i: away_group(ids, 3 - i, groups)),
            whole(rows, groups, state),
            whole(rows, heads),
            whole(rows, heads),
            table_spec,
        ],
        [slot_spec, bg_spec, sx_spec, sx_spec, sc_spec],
        [chunk, out(groups, rows, state), *[out(rows, 2 * heads)] * 2, out(EXTRA, 2 * heads)],
        far_memory(features, bmat, step_size, log_decay, table),
        [pltpu.VMEM((rows * groups, state), F32)],
    )
    far32 = exchange(away32, 1, count)
    (away10,) = call(
        second_kernel,
        2,
        [
            block(lambda ids, i: away_group(ids, 1 - i, groups)),
            bg_spec,
            sx_spec,
            sc_spec,
            table_spec,
        ],
        [slot_spec],
        [chunk],
        (features, bg, sx, sc, table),
    )
    far10 = exchange(away10, 1, count)

    def home(slot, far, earlier):
        def kernel(ids, *refs):
            home_kernel(slot, ids, *refs[:6], *refs[6 + len(earlier) :])

        half_spec = pl.BlockSpec((1, tall, width), lambda i, ids: (3 - slot + i, 0, 0))

        return call(
            kernel,
            2,
            [
                block(lambda ids, i: home_group(ids, slot - i, groups)),
                bg_spec,
                sx_spec,
                sc_spec,
                table_spec,
                slot_spec,
            ]
            + [ANY] * len(earlier),
            [half_spec, whole(tall, width), whole(tall, width)],
            [out(PLANE, tall, width), out(tall, width), out(tall, width)],
            (features, bg, sx, sc, table, far, *earlier),
            aliases={7: 0} if earlier else {},
        )

    own, piece3, piece2 = home(3, far32, ())
    moved3 = exchange(piece3, 6, count)
    moved2 = exchange(piece2, 4, count)
    own, piece1, piece0 = home(1, far10, (own,))
    pieces = [piece0, exchange(piece1, 2, count), moved2, moved3]

    group_block = pl.BlockSpec((1, rows, width), lambda i, ids: (i, 0, 0))
    y, r, cg = call(
        local_kernel,
        groups,
        [block(lambda ids, i: i), whole(rows, groups, state), bg_spec]
        + [sx_spec, sx_spec, sc_spec, table_spec],
        [group_block, group_block, pl.BlockSpec((1, rows, state), lambda i, ids: (i, 0, 0))],
        [out(groups, rows, width, kind=F32)] * 2 + [out(groups, rows, state)],
        (features, cmat, bg, sx, sr, sc, table),
        [pltpu.VMEM((rows * groups, state), F32)],
        cost=4,
        grant=14,
    )

    def gate(slot, earlier, after):
        def place(ids, i):
            return (ids[CORE] ^ (i & 1)) * (groups // 2) + (ids[CHIP] ^ (slot + i // 2))

        return call(
            lambda ids, gate_ref, *refs: gate_kernel(gate_ref, refs[-1]),
            4,
            [block(place)] + [ANY] * (len(earlier) + 1),
            [pl.BlockSpec((1, rows, width), lambda i, ids: (place(ids, i), 0, 0))],
            [out(groups, rows, width, kind=F32)],
            (*far_memory(gate_input), *earlier, after),
            aliases={2: 0} if earlier else {},
        )

    quarters = small_call(
        plane_down_kernel,
        ids,
        pieces,
        [out(tall, width // PLANE)] * PLANE,
        [pltpu.VMEM((PLANE, tall, width), BF16), pltpu.VMEM((PLANE, tall, width // PLANE), BF16)],
        [y],
    )
    sides = exchange_pieces(quarters, 8, count)
    skip, _ = lax.optimization_barrier((skip, quarters[0]))
    skips = [skip]
    for m in range(1, heads // skip.shape[0]):
        skips.append(exchange(skip, m, count))
    skips = [v.reshape(1, v.shape[0]) for v in skips]
    lacking, _ = lax.optimization_barrier((own, quarters[0]))
    lacking = lax.ppermute(lacking, AXES, [(i, i + 1) for i in range(0, count, 2)])
    side_scratch = [
        pltpu.VMEM((PLANE, tall, width // PLANE), BF16),
        pltpu.VMEM((PLANE, state, width // PLANE), BF16),
    ]
    enter = []
    stride = 2 * PLANE * PLANE
    if count > stride:
        (total,) = small_call(
            side_total_kernel, ids, sides, [out(tall, width // PLANE)], side_scratch[:1]
        )
        enter = [scan_groups(total, stride, count)]
    entering = small_call(
        side_up_kernel,
        ids,
        [*sides, *enter],
        [out(state, width // PLANE)] * PLANE,
        side_scratch,
    )
    gates = gate(0, (), entering[0])
    entering = exchange_pieces(entering, 8, count)
    states = small_call(
        plane_up_kernel,
        ids,
        (*entering, *pieces),
        [out(state, width)] * PLANE,
        [
            pltpu.VMEM((PLANE, tall, width), BF16),
            pltpu.VMEM((PLANE, state, width), BF16),
            pltpu.VMEM((PLANE, state, width // PLANE), BF16),
        ],
        [*gates, lacking],
    )
    states = exchange_pieces(states, 2, count)
    (skip_rows,) = small_call(
        skip_kernel, ids, skips, [out(groups, EXTRA, width, kind=F32)], (), [states[0]]
    )
    gain = norm_gain.reshape(1, inner)
    forwarded = []
    for s in states:
        forwarded.append(exchange(s, 1, count))

    def finish(entries, result):
        def kernel(*refs):
            finish_kernel([(m, side, (3 - m) % (4 if side else 2)) for m, side in entries], *refs)

        given = [forwarded[m] if side else states[m] for m, side in entries]
        updates = [lacking if side else far32 if m > 1 else far10 for m, side in entries]
        earlier = [] if result is None else [result]
        args = (ids, features, y, r, gates, cg, gain, skip_rows, *given, *updates)
        return pl.pallas_call(
            kernel,
            out_shape=out(rows, inner),
            in_specs=[SM] + [VM] * (len(args) - 1) + [ANY] * len(earlier),
            out_specs=ANY,
            scratch_shapes=[
                pltpu.VMEM((len(entries), state, width), BF16),
                pltpu.VMEM((len(entries), rows, width), BF16),
                pltpu.SemaphoreType.DMA((len(entries), rows // SUB)),
            ],
            input_output_aliases={len(args): 0} if earlier else {},
            compiler_params=pltpu.CompilerParams(vmem_limit_bytes=12 * MIB),
            cost_estimate=pl.CostEstimate(flops=10**9, bytes_accessed=4 * 2**20, transcendentals=0),
        )(*args, *earlier)

    (gates,) = gate(2, gates, states[0])
    result = finish([(0, 0), (0, 1)], None)
    result = finish([(3, 0)], result)
    result = finish([(2, 0), (1, 0), (3, 1), (2, 1)], result)
    return finish([(1, 1)], result)


def solution(mesh):
    return jax.shard_map(
        shards,
        mesh=mesh,
        in_specs=(
            P(("seq", "head"), None),
            P(("seq", "head"), None),
            P(("seq", "head"), None, None),
            P(("seq", "head"), None, None),
            P(("seq", "head"), None),
            P(("seq", "head"), None),
            P("head"),
            P(),
        ),
        out_specs=P(("seq", "head"), None),
        check_vma=False,
    )
```

```python
import jax
import jax.numpy as jnp
import numpy as np
from jax import lax
from jax.experimental import pallas as pl
from jax.experimental.pallas import tpu as pltpu
from jax.sharding import PartitionSpec as P

SUB = 128
MID = SUB // 2 - 1
EXTRA = 8
PLANE = 4
AXES = ("seq", "head")
MIB = 2**20
F32, BF16 = jnp.float32, jnp.bfloat16
VM = pl.BlockSpec(memory_space=pltpu.VMEM)
SM = pl.BlockSpec(memory_space=pltpu.SMEM)
ANY = pl.BlockSpec(memory_space=pl.ANY)
CORE, CHIP, SIDE = 0, 1, 2


def split_two(value):
    high = value.astype(BF16)
    return high, (value - high.astype(F32)).astype(BF16)


def dot(a, b):
    return lax.dot_general(a, b, (((1,), (0,)), ((), ())), preferred_element_type=F32)


def dot_tn(a, b):
    return lax.dot_general(a, b, (((0,), (0,)), ((), ())), preferred_element_type=F32)


def dot_nt(a, b):
    return lax.dot_general(a, b, (((1,), (1,)), ((), ())), preferred_element_type=F32)


def spread_table(heads, groups, width):
    per_group = heads // groups
    row = np.arange(3 * heads - per_group)[:, None] % heads
    column = np.arange(width)[None, :] // (width // per_group)
    return jnp.asarray(row == heads - per_group + column, BF16)


def spread_of(table_ref, group, heads, groups):
    per_group = heads // groups
    start = pl.multiple_of(per_group * (groups - 1 - group), per_group)
    return table_ref[pl.ds(start, 2 * heads), :]


def pair_row(later, earlier, subs):
    return 1 + 2 * subs + later * (later - 1) // 2 + earlier


def decay_of(ref):
    rows = ref[-EXTRA:, :].astype(F32)
    return rows[0:1] + rows[1:2]


def put_decay(ref, decay):
    high, low = split_two(decay)
    row = lax.broadcasted_iota(jnp.int32, (EXTRA, decay.shape[1]), 0)
    both = jnp.where(row == 0, high.astype(F32), jnp.where(row == 1, low.astype(F32), 0.0))
    ref[-EXTRA:, :] = both.astype(BF16)


def write_scales(decay_ref, step_ref, sx_ref, sr_ref, sc_ref):
    rows, heads = decay_ref.shape
    subs = rows // SUB
    decay = decay_ref[...]
    high = decay.astype(BF16)
    rest = decay - high.astype(F32)
    mid = rest.astype(BF16)
    low = (rest - mid.astype(F32)).astype(BF16)
    row = lax.broadcasted_iota(jnp.int32, (rows, rows), 0)
    column = lax.broadcasted_iota(jnp.int32, (rows, rows), 1)
    lower = (row >= column).astype(BF16)
    cum = dot(lower, high) + dot(lower, mid) + dot(lower, low)
    centre = [cum[b * SUB + MID : b * SUB + MID + 1] for b in range(subs)]
    last = cum[rows - 1 : rows]
    for b in range(subs):
        part = slice(b * SUB, (b + 1) * SUB)
        off = cum[part] - centre[b]
        high, low = split_two(jnp.exp(-off) * step_ref[part, :])
        sx_ref[part, :heads] = high
        sx_ref[part, heads:] = low
        high, low = split_two(jnp.exp(off))
        sr_ref[part, :heads] = high
        sr_ref[part, heads:] = low
    scalars = [last] + [last - c for c in centre] + centre
    for b in range(subs):
        scalars += [centre[b] - centre[a] for a in range(b)]
    pad = jnp.zeros((EXTRA - len(scalars), heads), F32)
    high, low = split_two(jnp.exp(jnp.concatenate(scalars + [pad], axis=0)))
    sc_ref[:, :heads] = high
    sc_ref[:, heads:] = low


def scaled_features(x, sx_ref, spread):
    return (x.astype(F32) * dot(sx_ref[...], spread)).astype(BF16)


def rows_of(ref, group, groups):
    return ref[pl.ds(group, ref.shape[0] // groups, stride=groups), :].astype(BF16)


def columns_of(group, width):
    return pl.ds(pl.multiple_of(group * width, width), width)


def update_of(xa, b_group, scalars):
    total = None
    for b in range(xa.shape[0] // SUB):
        part = slice(b * SUB, (b + 1) * SUB)
        term = dot_tn(b_group[part], xa[part]) * scalars[1 + b : 2 + b]
        total = term if total is None else total + term
    return total


def own_update(group, groups, x, b_ref, sx_ref, sc_ref, table_ref):
    spread = spread_of(table_ref, group, sx_ref.shape[1] // 2, groups)
    scalars = dot(sc_ref[...], spread)
    xa = scaled_features(x, sx_ref, spread)
    return update_of(xa, rows_of(b_ref, group, groups), scalars), scalars[0:1]


def away_group(ids, slot, groups):
    return (1 - ids[CORE]) * (groups // 2) + (ids[CHIP] ^ slot)


def home_group(ids, slot, groups):
    return ids[CORE] * (groups // 2) + (ids[CHIP] ^ slot)


def put_update(ref, update, decay):
    ref[:-EXTRA, :] = update.astype(BF16)
    put_decay(ref, decay)


def first_kernel(slots, ids, x_far, b_far, step_far, decay_far, table_far, *refs):
    u_ref, b32, sx_ref, sr_ref, sc_ref, x_ref, b_ref, step_ref, decay_ref, table_ref, sems = refs
    rows, groups, state = b_ref.shape
    width = x_ref.shape[2]
    places = [away_group(ids, m, groups) for m in slots]
    pairs = [(decay_far, decay_ref), (step_far, step_ref), (b_far, b_ref), (table_far, table_ref)]
    pairs += [(x_far.at[:, columns_of(g, width)], x_ref.at[i]) for i, g in enumerate(places)]
    copies = [pltpu.make_async_copy(a, b, sems.at[i]) for i, (a, b) in enumerate(pairs)]
    for copy in copies:
        copy.start()
    copies[0].wait()
    copies[1].wait()
    write_scales(decay_ref, step_ref, sx_ref, sr_ref, sc_ref)
    copies[2].wait()
    b32[...] = b_ref[...].astype(F32).reshape(rows * groups, state)
    copies[3].wait()
    for i, group in enumerate(places):
        copies[4 + i].wait()
        put_update(
            u_ref.at[i], *own_update(group, groups, x_ref[i], b32, sx_ref, sc_ref, table_ref)
        )


def second_kernel(slots, groups, ids, x_ref, b_ref, sx_ref, sc_ref, table_ref, u_ref):
    for i, m in enumerate(slots):
        group = away_group(ids, m, groups)
        x = x_ref[:, columns_of(group, u_ref.shape[2])]
        put_update(u_ref.at[i], *own_update(group, groups, x, b_ref, sx_ref, sc_ref, table_ref))


def home_kernel(slots, groups, ids, x_ref, b_ref, sx_ref, sc_ref, table_ref, far_ref, u_ref, *outs):
    late = ids[CORE].astype(F32)
    for i, m in enumerate(slots):
        group = home_group(ids, m, groups)
        x = x_ref[:, columns_of(group, u_ref.shape[2])]
        update, decay = own_update(group, groups, x, b_ref, sx_ref, sc_ref, table_ref)
        put_update(u_ref.at[i], update, decay)
        far, far_decay = far_ref[i, :-EXTRA, :].astype(F32), decay_of(far_ref.at[i])
        joined = update * (late + (1.0 - late) * far_decay) + far * ((1.0 - late) + late * decay)
        put_update(outs[i], joined, decay * far_decay)


def skip_kernel(ids, *refs):
    pieces, out_ref = refs[:-1], refs[-1]
    groups, _, width = out_ref.shape
    share = pieces[0].shape[1]
    heads = share * len(pieces)
    own = 2 * ids[CHIP] + ids[CORE]
    place = own & (len(pieces) - 1)
    row = lax.broadcasted_iota(jnp.int32, (share, width), 0)
    column = lax.broadcasted_iota(jnp.int32, (share, width), 1) // (width * groups // heads)
    spread_groups = share * groups // heads
    for m, piece in enumerate(pieces):
        high, low = split_two(jnp.broadcast_to(piece[...], (EXTRA, share)))
        for k in range(spread_groups):
            pick = (row == column + k * (heads // groups)).astype(BF16)
            out_ref[(place ^ m) * spread_groups + k] = dot(high, pick) + dot(low, pick)


def gate_kernel(ids, gate_ref, out_ref):
    groups, _, width = out_ref.shape
    for group in range(groups):
        half = 0.5 * gate_ref[:, group * width : (group + 1) * width].astype(F32)
        out_ref[group] = half + half * jnp.tanh(half)


def local_kernel(
    ids, x_ref, c_ref, b_ref, sx_ref, sr_ref, sc_ref, table_ref, y_ref, r_ref, cg_ref, c32
):
    rows, groups, state = c_ref.shape
    width = y_ref.shape[2]
    heads = sx_ref.shape[1] // 2
    subs = rows // SUB
    c32[...] = c_ref[...].astype(F32).reshape(rows * groups, state)
    row = lax.broadcasted_iota(jnp.int32, (SUB, SUB), 0)
    column = lax.broadcasted_iota(jnp.int32, (SUB, SUB), 1)

    def one(group, carry):
        c_group = rows_of(c32, group, groups)
        cg_ref[group] = c_group
        spread = spread_of(table_ref, group, heads, groups)
        scalars = dot(sc_ref[...], spread)
        xa = scaled_features(x_ref[:, columns_of(group, width)], sx_ref, spread)
        row_scale = dot(sr_ref[...], spread)
        b_group = rows_of(b_ref, group, groups)
        for b in range(subs):
            part = slice(b * SUB, (b + 1) * SUB)
            scores = jnp.where(row >= column, dot_nt(c_group[part], b_group[part]), 0.0)
            inner = dot(scores.astype(BF16), xa[part])
            for a in range(b):
                other = slice(a * SUB, (a + 1) * SUB)
                scores = dot_nt(c_group[part], b_group[other]).astype(BF16)
                at = pair_row(b, a, subs)
                inner = inner + dot(scores, xa[other]) * scalars[at : at + 1]
            y_ref[group, part, :] = row_scale[part] * inner
            r_ref[group, part, :] = row_scale[part] * scalars[1 + subs + b : 2 + subs + b]
        return carry

    lax.fori_loop(0, groups, one, 0)


def hold(held, place, pieces):
    for m, piece in enumerate(pieces):
        held[place ^ m] = piece[...]


def fold(held):
    total, decay = held[0, :-EXTRA, :].astype(F32), decay_of(held.at[0])
    for k in range(1, PLANE):
        d = decay_of(held.at[k])
        total = d * total + held[k, :-EXTRA, :].astype(F32)
        decay = d * decay
    return total, decay


def plane_down_kernel(ids, p0, p1, p2, p3, *refs):
    o0, o1, o2, o3, held, cut = refs[-6:]
    hold(held, ids[CHIP], (p0, p1, p2, p3))
    total, decay = fold(held)
    quarter = total.shape[1] // PLANE
    for k in range(PLANE):
        part = slice(k * quarter, (k + 1) * quarter)
        put_update(cut.at[k], total[:, part], decay[:, part])
    for m, out in enumerate((o0, o1, o2, o3)):
        out[...] = cut[ids[SIDE] ^ m]


def side_total_kernel(ids, p0, p1, p2, p3, out_ref, held):
    hold(held, ids[SIDE], (p0, p1, p2, p3))
    put_update(out_ref, *fold(held))


def side_up_kernel(ids, p0, p1, p2, p3, *refs):
    o0, o1, o2, o3, held, state = refs[-6:]
    hold(held, ids[SIDE], (p0, p1, p2, p3))
    if len(refs) == 7:
        state[0] = refs[0][:-EXTRA, :]
    else:
        state[0] = jnp.zeros(state.shape[1:], BF16)
    states_after(held, state)
    for m, out in enumerate((o0, o1, o2, o3)):
        out[...] = state[ids[SIDE] ^ m]


def states_after(held, state):
    now = state[0].astype(F32)
    for k in range(1, PLANE):
        now = decay_of(held.at[k - 1]) * now + held[k - 1, :-EXTRA, :].astype(F32)
        state[k] = now.astype(BF16)


def plane_up_kernel(ids, e0, e1, e2, e3, p0, p1, p2, p3, *refs):
    o0, o1, o2, o3, held, state, enter = refs[-7:]
    quarter = e0.shape[1]
    hold(held, ids[CHIP], (p0, p1, p2, p3))
    for m, piece in enumerate((e0, e1, e2, e3)):
        enter[ids[SIDE] ^ m] = piece[...]
    for k in range(PLANE):
        state[0, :, k * quarter : (k + 1) * quarter] = enter[k]
    states_after(held, state)
    for m, out in enumerate((o0, o1, o2, o3)):
        out[...] = state[ids[CHIP] ^ m]


def small_call(kernel, ids, args, outs, scratch=(), after=(), far=(), reuse=0, cost=0, grant=8):
    size = sum(a.size * 2 for a in (*args, *far)) + sum(2 * o.size for o in outs)

    def body(ids, *refs):
        given = len(far) + len(args)
        kernel(ids, *refs[:given], *refs[given + len(after) :])

    return pl.pallas_call(
        body,
        out_shape=outs,
        in_specs=[SM] + [ANY] * len(far) + [VM] * len(args) + [ANY] * len(after),
        out_specs=[VM] * len(outs),
        scratch_shapes=list(scratch),
        input_output_aliases={1 + len(far) + len(args) + n: n for n in range(reuse)},
        compiler_params=pltpu.CompilerParams(vmem_limit_bytes=grant * MIB),
        cost_estimate=pl.CostEstimate(
            flops=size + cost * 10**9, bytes_accessed=size, transcendentals=0
        ),
    )(ids, *far, *args, *after)


def exchange(value, mask, count):
    return lax.ppermute(value, AXES, [(i, i ^ mask) for i in range(count)])


def exchange_pieces(pieces, mask, count):
    moved = {}
    for m in (3, 2, 1):
        moved[m] = exchange(pieces[m], mask * m, count)
    return [pieces[0], moved[1], moved[2], moved[3]]


def shifted(value, steps, count):
    return lax.ppermute(value, AXES, [(i, i + steps) for i in range(count - steps)])


def scan_groups(total, stride, count):
    places = count // stride

    def parts(message):
        decay = message[-EXTRA].astype(F32) + message[-EXTRA + 1].astype(F32)
        return message[:-EXTRA].astype(F32), decay

    def packed(value, decay):
        high, low = split_two(decay)
        rest = jnp.zeros((EXTRA - 2, decay.shape[0]), BF16)
        return jnp.concatenate([value.astype(BF16), high[None], low[None], rest], axis=0)

    covered = shifted(total, stride, count)
    reach = 1
    while reach < places - 1:
        value, decay = parts(covered)
        own, own_decay = parts(total)
        longer = packed(own_decay[None] * value + own, own_decay * decay)
        far, far_decay = parts(shifted(longer, stride * (reach + 1), count))
        covered = packed(decay[None] * far + value, decay * far_decay)
        reach = 2 * reach + 1
    return covered


def finish_kernel(entries, ids, x_ref, y_ref, r_ref, gate_ref, cg_ref, gain_ref, skip_ref, *refs):
    count = len(entries)
    states, updates = refs[:count], refs[count : 2 * count]
    out_ref, held, made, sems = refs[-4:]
    groups, rows, width = y_ref.shape
    copies = []
    for n, (slot, side, at) in enumerate(entries):
        group = (ids[CORE] ^ side) * (groups // 2) + (ids[CHIP] ^ slot)

        @pl.when(ids[CORE] == 0)
        def _():
            held[n] = states[n][...]

        @pl.when(ids[CORE] == 1)
        def _():
            after = decay_of(updates[n].at[at]) * states[n][...].astype(F32)
            held[n] = (after + updates[n][at, :-EXTRA, :].astype(F32)).astype(BF16)

        columns = pl.ds(pl.multiple_of(group * width, width), width)
        gain, skip = gain_ref[:, columns], skip_ref[group, 0:1, :]
        for b in range(rows // SUB):
            part = slice(b * SUB, (b + 1) * SUB)
            carried = dot(cg_ref[group, part, :], held[n])
            ssm = y_ref[group, part, :] + r_ref[group, part, :] * carried
            ssm = (ssm + skip * x_ref[part, columns].astype(F32)).astype(BF16)
            gated = ssm.astype(F32) * gate_ref[group, part, :]
            mean = jnp.mean(gated * gated, axis=1, keepdims=True)
            made[n, part, :] = (gated * lax.rsqrt(mean + 1e-05) * gain).astype(BF16)
            copies.append(
                pltpu.make_async_copy(
                    made.at[n, part, :], out_ref.at[part, columns], sems.at[n, b]
                )
            )
            copies[-1].start()
    for copy in copies:
        copy.wait()


def shards(features, gate_input, bmat, cmat, step_size, log_decay, skip, norm_gain):
    rows, inner = features.shape
    groups, state = bmat.shape[1:]
    heads = step_size.shape[1]
    width = inner // groups
    count = lax.axis_size("seq") * lax.axis_size("head")
    me = lax.axis_index("seq") * lax.axis_size("head") + lax.axis_index("head")
    ids = jnp.stack([me & 1, (me >> 1) & (PLANE - 1), (me >> 3) & (PLANE - 1)]).astype(jnp.int32)
    tall = state + EXTRA
    table = spread_table(heads, groups, width)

    def far_memory(*values):
        return tuple(pltpu.with_memory_space_constraint(v, pltpu.HBM) for v in values)


    def out(*shape, kind=BF16):
        return jax.ShapeDtypeStruct(shape, kind)

    rows_kind, scale_kind = out(rows * groups, state, kind=F32), out(rows, 2 * heads)
    piece = out(tall, width)
    head_slots, rest_slots = (3,), (2, 1, 0)

    def bound(kernel, *given):
        return lambda *refs: kernel(*given, *refs)

    away3, b_rows, sx, sr, sc = small_call(
        bound(first_kernel, head_slots),
        ids,
        (),
        [out(1, tall, width), rows_kind, scale_kind, scale_kind, out(EXTRA, 2 * heads)],
        [
            pltpu.VMEM((1, rows, width), BF16),
            pltpu.VMEM((rows, groups, state), BF16),
            pltpu.VMEM((rows, heads), F32),
            pltpu.VMEM((rows, heads), F32),
            pltpu.VMEM(table.shape, BF16),
            pltpu.SemaphoreType.DMA((5,)),
        ],
        far=far_memory(features, bmat, step_size, log_decay, table),
        cost=1,
        grant=10,
    )
    far3 = exchange(away3, 1, count)
    (away210,) = small_call(
        bound(second_kernel, rest_slots, groups),
        ids,
        (features, b_rows, sx, sc, table),
        [out(3, tall, width)],
        cost=1,
    )
    far210 = exchange(away210, 1, count)

    def home(slots, far):
        return small_call(
            bound(home_kernel, slots, groups),
            ids,
            (features, b_rows, sx, sc, table, far),
            [out(len(slots), tall, width)] + [piece] * len(slots),
            cost=1,
        )

    own3, piece3 = home(head_slots, far3)
    moved3 = exchange(piece3, 6, count)
    own210, piece2, piece1, piece0 = home(rest_slots, far210)
    moved2 = exchange(piece2, 4, count)
    moved1 = exchange(piece1, 2, count)
    pieces = [piece0, moved1, moved2, moved3]

    large = out(groups, rows, width, kind=F32)
    y, r, cg = small_call(
        local_kernel,
        ids,
        (features, cmat, b_rows, sx, sr, sc, table),
        [large, large, out(groups, rows, state)],
        [pltpu.VMEM((rows * groups, state), F32)],
        cost=4,
        grant=10,
    )

    quarters = small_call(
        plane_down_kernel,
        ids,
        pieces,
        [out(tall, width // PLANE)] * PLANE,
        [pltpu.VMEM((PLANE, tall, width), BF16), pltpu.VMEM((PLANE, tall, width // PLANE), BF16)],
        [y],
    )
    sides = exchange_pieces(quarters, 8, count)
    skip, _ = lax.optimization_barrier((skip, quarters[0]))
    skips = [skip]
    for m in range(1, heads // skip.shape[0]):
        skips.append(exchange(skip, m, count))
    skips = [v.reshape(1, v.shape[0]) for v in skips]
    early = [(i, i + 1) for i in range(0, count, 2)]
    lack3, lack210, _ = lax.optimization_barrier((own3, own210, quarters[0]))
    lack3, lack210 = (lax.ppermute(v, AXES, early) for v in (lack3, lack210))
    side_scratch = [
        pltpu.VMEM((PLANE, tall, width // PLANE), BF16),
        pltpu.VMEM((PLANE, state, width // PLANE), BF16),
    ]
    enter = []
    stride = 2 * PLANE * PLANE
    if count > stride:
        (total,) = small_call(
            side_total_kernel, ids, sides, [out(tall, width // PLANE)], side_scratch[:1]
        )
        enter = [scan_groups(total, stride, count)]
    entering = small_call(
        side_up_kernel,
        ids,
        [*sides, *enter],
        [out(state, width // PLANE)] * PLANE,
        side_scratch,
    )
    (gates,) = small_call(gate_kernel, ids, (gate_input,), [large], after=[entering[0]], cost=2)
    (skip_rows,) = small_call(
        skip_kernel, ids, skips, [out(groups, EXTRA, width, kind=F32)], (), [entering[0]]
    )
    entering = exchange_pieces(entering, 8, count)
    states = small_call(
        plane_up_kernel,
        ids,
        (*entering, *pieces),
        [out(state, width)] * PLANE,
        [
            pltpu.VMEM((PLANE, tall, width), BF16),
            pltpu.VMEM((PLANE, state, width), BF16),
            pltpu.VMEM((PLANE, state, width // PLANE), BF16),
        ],
        [gates, skip_rows, lack3, lack210],
    )
    states = exchange_pieces(states, 2, count)
    gain = norm_gain.reshape(1, inner)
    forwarded = []
    for s in states:
        forwarded.append(exchange(s, 1, count))

    def finish(entries, result):
        def kernel(*refs):
            finish_kernel([(m, side, max(0, 2 - m)) for m, side in entries], *refs)

        given = [forwarded[m] if side else states[m] for m, side in entries]
        updates = [((far210, far3), (lack210, lack3))[side][m == 3] for m, side in entries]
        earlier = [] if result is None else [result]
        args = (ids, features, y, r, gates, cg, gain, skip_rows, *given, *updates)
        return pl.pallas_call(
            kernel,
            out_shape=out(rows, inner),
            in_specs=[SM] + [VM] * (len(args) - 1) + [ANY] * len(earlier),
            out_specs=ANY,
            scratch_shapes=[
                pltpu.VMEM((len(entries), state, width), BF16),
                pltpu.VMEM((len(entries), rows, width), BF16),
                pltpu.SemaphoreType.DMA((len(entries), rows // SUB)),
            ],
            input_output_aliases={len(args): 0} if earlier else {},
            compiler_params=pltpu.CompilerParams(vmem_limit_bytes=12 * MIB),
            cost_estimate=pl.CostEstimate(flops=10**9, bytes_accessed=4 * 2**20, transcendentals=0),
        )(*args, *earlier)

    result = finish([(0, 0)], None)
    result = finish([(0, 1), (1, 0)], result)
    result = finish([(1, 1), (2, 0)], result)
    result = finish([(2, 1), (3, 0)], result)
    return finish([(3, 1)], result)


def solution(mesh):
    return jax.shard_map(
        shards,
        mesh=mesh,
        in_specs=(
            P(("seq", "head"), None),
            P(("seq", "head"), None),
            P(("seq", "head"), None, None),
            P(("seq", "head"), None, None),
            P(("seq", "head"), None),
            P(("seq", "head"), None),
            P("head"),
            P(),
        ),
        out_specs=P(("seq", "head"), None),
        check_vma=False,
    )
```
